768 devices in a mesh: dp: 48 (over z, y_hi, core), ctx: 16 (over x, y_lo).
Axes of the slice: x: 4, y: 8 (y_hi: 2, y_lo: 4; y = y_hi * 4 + y_lo), z: 12, core: 2. Of those that a mesh axis runs over, the one named last changes fastest.
Arguments:
- queries: bfloat16 [48, 2048, 1152], P('dp', 'ctx')
- key_states: bfloat16 [48, 2048, 1152], P('dp', 'ctx')
- value_states: bfloat16 [48, 2048, 1152], P('dp', 'ctx'), may hold values from -6 to 6
- out_cotangent: bfloat16 [48, 2048, 1024], P('dp', 'ctx'), may hold values from -0.875 to 0.875
- out_weight: bfloat16 [1024, 1152], replicated, may hold values from -3 to 3
- block_clip: int32 [48, 16], P('dp', 'ctx'), may hold values from 0 to 3, never falling along the last dimension, each value on 1 to 13 neighbouring positions
Outputs:
- sublayer_out: bfloat16 [48, 2048, 1024], P('dp', 'ctx')
- query_grad: bfloat16 [48, 2048, 1152], P('dp', 'ctx')
- key_grad: bfloat16 [48, 2048, 1152], P('dp', 'ctx')
- value_grad: bfloat16 [48, 2048, 1152], P('dp', 'ctx')
- weight_grad: float32 [1024, 1152], P('ctx', 'dp')
The draws below stay inside these ranges and needn't reach their ends.
All inputs are finite; a program needn't handle non-finite values.
Results may differ from the reference program's by a relative error of at most 0.034.
Values may be sent and summed in bfloat16 or wider, within the bound.
A program may use at most 32 MiB of HBM per device.

```python
import math
import jax
import jax.numpy as jnp
import numpy as np
from jax import lax

HEADS = 18
HDIM = 64
HD = 1152
DOUT = 1024
BLOCK = 128
WIN = 256
TOK_DEV = 128
LENGTH = 2048
SEQS = 48
NBLK = 16
CLIPS = 4
CLIP_MOST = 13
N_CTX = 16


def paired_rows(key):
    shape = (SEQS, LENGTH, HEADS * HDIM)
    base_query = jnp.clip(jax.random.normal(jax.random.fold_in(key, 101), shape, jnp.float32), -6.0, 6.0)
    base_key = jnp.clip(jax.random.normal(jax.random.fold_in(key, 202), shape, jnp.float32), -6.0, 6.0)
    return (base_query, base_key)


def draw_queries(key, part):
    return paired_rows(key)[0].astype(jnp.bfloat16)


def draw_key_states(key, part):
    return paired_rows(key)[1].astype(jnp.bfloat16)


def strengthened(result, key, source, target, shards_of, factor):
    def block_of(dim):
        return (jnp.arange(result.shape[dim]) // (result.shape[dim] // shards_of)).reshape((-1,) + (1,) * (result.ndim - 1 - dim))

    near = jax.random.permutation(key, shards_of)[block_of(target)]
    second = (block_of(target) + shards_of // 2) % shards_of
    return jnp.where((block_of(source) == near) | (block_of(source) == second), factor * result, result)


def shard_levels(rng, shape, split, smallest, top_value):
    def one(position, blocks):
        heights = jax.random.uniform(jax.random.fold_in(jax.random.fold_in(rng, 6), position), (blocks,), jnp.float32, smallest / len(split), top_value / len(split))
        return jnp.repeat(jnp.exp(heights), shape[position] // blocks).reshape((-1,) + (1,) * (len(shape) - position - 1))

    gain = one(*split[0])
    for cut in split[1:]:
        gain = gain * one(*cut)
    return gain


def profile(amount, total, most, lean):
    portions = [(1 << 20) // math.isqrt(rank ** lean) + 1 for rank in range(2, amount + 1)]
    spare, given = total - most - (amount - 1), [1] * (amount - 1)
    while spare > 0:
        free = [i for i in range(amount - 1) if given[i] < most]
        whole, budget = sum([portions[i] for i in free]), spare
        for i in free:
            more = min(most - given[i], max(1, budget * portions[i] // whole), spare)
            given[i] = given[i] + more
            spare = spare - more
    return np.array([most] + given)


def ragged(own_key, amount, total, bound, slope):
    if amount == 2:
        one = jax.random.randint(own_key, (), max(1, total - bound), min(bound, total - 1) + 1)
        return jnp.stack([one, total - one])
    sizes = jnp.asarray(profile(amount, total, bound, slope), jnp.int32)
    pairs = (amount - 1) // 2
    donor, taker = sizes[1:1 + 2 * pairs:2], sizes[2:2 + 2 * pairs:2]
    room = jnp.minimum(donor - 1, bound - taker)
    moved = jax.random.randint(jax.random.fold_in(own_key, 1), (pairs,), 0, 1 << 20) % (room + 1)
    sizes = sizes.at[1:1 + 2 * pairs:2].set(donor - moved).at[2:2 + 2 * pairs:2].set(taker + moved)
    return sizes[jax.random.permutation(jax.random.fold_in(own_key, 2), amount)]


def bell_draw(stream_key, dims, deviation, bound, split=(), held_as=jnp.bfloat16):
    drawn = jax.random.normal(stream_key, dims, jnp.float32) * deviation
    if len(split) > 0:
        drawn = shard_levels(stream_key, dims, split, -0.22, 0.18) * drawn
    return jnp.clip(drawn, min=-bound, max=bound).astype(held_as)


def heavy_noise(own_key, extent, deviation, bound, shards, heavy, kind=jnp.bfloat16):
    result = deviation * jax.random.normal(own_key, extent, jnp.float32)
    if shards:
        result = result * shard_levels(own_key, extent, shards, -0.22, 0.18)
    return jnp.clip(strengthened(result, jax.random.fold_in(own_key, 3), *heavy), -bound, bound).astype(kind)


def setup_inputs(seed: int = 0) -> dict:
    key_list = jax.random.split(jax.random.key(seed), 7)
    queries = draw_queries(jax.random.fold_in(key_list[6], 71), 0)
    key_states = draw_key_states(jax.random.fold_in(key_list[6], 71), 0)
    value_states = bell_draw(key_list[2], (SEQS, LENGTH, HD), 1.0, 6.0, ((0, 48), (1, 16)))
    out_cotangent = heavy_noise(key_list[3], (SEQS, LENGTH, DOUT), 0.1, 0.875, ((0, 48), (1, 16)), (1, 2, 16, 2.0))
    out_weight = bell_draw(key_list[4], (DOUT, HD), (16.0 / HD ** 0.5), 3.0)
    block_clip = jax.vmap(lambda own: jnp.searchsorted(jnp.cumsum(ragged(own, CLIPS, NBLK, CLIP_MOST, 2)), jnp.arange(NBLK), side="right"))(jax.random.split(key_list[5], SEQS)).reshape((SEQS, NBLK)).astype(jnp.int32)
    return {"queries": queries, "key_states": key_states, "value_states": value_states, "out_cotangent": out_cotangent, "out_weight": out_weight, "block_clip": block_clip}


def split_heads(matrix):
    return matrix.reshape(matrix.shape[0], HEADS, HDIM).transpose(1, 0, 2)

def merge_heads(stacked):
    return stacked.transpose(1, 0, 2).reshape(stacked.shape[1], HEADS * HDIM)

def rounded_back(values):
    return lax.optimization_barrier(values.astype(jnp.bfloat16)).astype(jnp.float32)

def reference(queries, key_states, value_states, out_cotangent, out_weight, block_clip):
    scaling = 1.0 / math.sqrt(HDIM)
    width = HEADS * HDIM
    zero_rows = jnp.zeros((WIN, width), jnp.bfloat16)
    weight_f32 = out_weight

    def one_sequence(weight_sum, inputs):
        query_seq, key_seq, value_seq, cotangent_seq, clip_seq = inputs
        clip_steps = jnp.repeat(clip_seq, BLOCK).astype(jnp.int32)
        key_padded = jnp.concatenate([zero_rows, key_seq], axis=0)
        value_padded = jnp.concatenate([zero_rows, value_seq], axis=0)
        clip_padded = jnp.concatenate([jnp.full((WIN,), -1, jnp.int32), clip_steps], axis=0)

        def one_range(carry, index):
            key_acc, value_acc, weight_acc = carry
            start = (index * TOK_DEV).astype(jnp.int32)
            query_rows = lax.dynamic_slice_in_dim(query_seq, start, TOK_DEV, 0)
            cotangent_rows = lax.dynamic_slice_in_dim(cotangent_seq, start, TOK_DEV, 0)
            key_rows = lax.dynamic_slice_in_dim(key_padded, start, TOK_DEV + WIN, 0)
            value_rows = lax.dynamic_slice_in_dim(value_padded, start, TOK_DEV + WIN, 0)
            query_clip = lax.dynamic_slice_in_dim(clip_steps, start, TOK_DEV, 0)
            key_clip = lax.dynamic_slice_in_dim(clip_padded, start, TOK_DEV + WIN, 0)
            query_pos = start + jnp.arange(TOK_DEV, dtype=jnp.int32)
            key_pos = start - WIN + jnp.arange(TOK_DEV + WIN, dtype=jnp.int32)
            visible = (key_pos[None, :] <= query_pos[:, None]) & (query_pos[:, None] - key_pos[None, :] < WIN)
            visible = visible & (key_pos[None, :] >= 0) & (query_clip[:, None] == key_clip[None, :])
            query_heads = split_heads(query_rows).astype(jnp.float32)
            key_heads = split_heads(key_rows).astype(jnp.float32)
            value_heads = split_heads(value_rows).astype(jnp.float32)
            scores = jnp.einsum('hqd,hkd->hqk', query_heads, key_heads) * scaling
            scores = jnp.where(visible[None], scores, -1e+30)
            maximum = lax.optimization_barrier(jnp.max(scores, axis=2, keepdims=True))
            log_total = maximum[:, :, 0] + jnp.log(lax.optimization_barrier(jnp.sum(jnp.exp(scores - maximum), axis=2)))
            probs = jnp.exp(scores - log_total[:, :, None])
            weights = probs.astype(jnp.bfloat16)
            attended = merge_heads(jnp.einsum('hqk,hkd->hqd', weights.astype(jnp.float32), value_heads)).astype(jnp.bfloat16)
            output_rows = jnp.dot(attended, weight_f32.T, preferred_element_type=jnp.float32).astype(jnp.bfloat16)
            d_attended = jnp.dot(cotangent_rows, weight_f32, preferred_element_type=jnp.float32).astype(jnp.bfloat16)
            d_heads = split_heads(d_attended).astype(jnp.float32)
            delta = lax.optimization_barrier(jnp.sum(d_heads * split_heads(attended).astype(jnp.float32), axis=2))
            d_weights = jnp.einsum('hqd,hkd->hqk', d_heads, value_heads)
            d_scores = (probs * (d_weights - delta[:, :, None]) * scaling).astype(jnp.bfloat16)
            query_grad = merge_heads(jnp.einsum('hqk,hkd->hqd', d_scores.astype(jnp.float32), key_heads)).astype(jnp.bfloat16)
            key_part = rounded_back(merge_heads(jnp.einsum('hqk,hqd->hkd', d_scores.astype(jnp.float32), query_heads)))
            value_part = rounded_back(merge_heads(jnp.einsum('hqk,hqd->hkd', weights.astype(jnp.float32), d_heads)))
            current_key = lax.dynamic_slice_in_dim(key_acc, start, TOK_DEV + WIN, 0)
            current_value = lax.dynamic_slice_in_dim(value_acc, start, TOK_DEV + WIN, 0)
            key_acc = lax.dynamic_update_slice_in_dim(key_acc, current_key + key_part, start, 0)
            value_acc = lax.dynamic_update_slice_in_dim(value_acc, current_value + value_part, start, 0)
            weight_part = rounded_back(jnp.dot(cotangent_rows.T, attended, preferred_element_type=jnp.float32))
            return ((key_acc, value_acc, weight_acc + weight_part), (output_rows, query_grad))
        start_acc = jnp.zeros((WIN + LENGTH, width), jnp.float32)
        indices = jnp.arange(N_CTX, dtype=jnp.int32)
        (key_acc, value_acc, weight_sum), (output_rows, query_grad) = lax.scan(one_range, (start_acc, start_acc, weight_sum), indices)
        results = (output_rows.reshape(LENGTH, DOUT), query_grad.reshape(LENGTH, width), key_acc[WIN:].astype(jnp.bfloat16), value_acc[WIN:].astype(jnp.bfloat16))
        return (weight_sum, results)
    weight_start = jnp.zeros((DOUT, width), jnp.float32)
    weight_grad, (sublayer_out, query_grad, key_grad, value_grad) = lax.scan(one_sequence, weight_start, (queries, key_states, value_states, out_cotangent, block_clip))
    return (sublayer_out, query_grad, key_grad, value_grad, weight_grad)
```

```python
import math

import jax
import jax.numpy as jnp
from jax import lax
from jax.experimental import pallas as pl
from jax.experimental.pallas import tpu as pltpu
from jax.sharding import PartitionSpec as P

HDIM = 64
BLOCK = 128
WIN = 256
GROUPS = 3
PAIR = 2 * HDIM

NZ, NYH, NC = 12, 2, 2
NX, NYL = 4, 4

BF16 = jnp.bfloat16
F32 = jnp.float32
MESH = pl.DeviceIdType.MESH


def dot_nn(a, b):
    return lax.dot_general(a, b, (((1,), (0,)), ((), ())), preferred_element_type=F32)


def dot_nt(a, b):
    return lax.dot_general(a, b, (((1,), (1,)), ((), ())), preferred_element_type=F32)


def dot_tn(a, b):
    return lax.dot_general(a, b, (((0,), (0,)), ((), ())), preferred_element_type=F32)


def kernel(
    clip_ref, q_ref, k_ref, v_ref, cot_ref, w_ref,
    out_ref, dq_ref, dk_ref, dv_ref, wg_ref,
    kcat, vcat, clips, bias, da_buf, att_buf,
    own_k, own_v, near_k, near_v, far_k, far_v, sum_k, sum_v,
    in_far_k, in_far_v, in_near_k, in_near_v,
    g_buf, a_in, b_buf, b_in, z_buf, z_in, y_buf, y_in, t_buf,
    clip_sem, halo_sem, back_sem, a_sem, b_sem, z_send, z_recv, y_send, y_recv,
):
    dp, ctx = lax.axis_index("dp"), lax.axis_index("ctx")
    n_ctx = NX * NYL
    core = lax.rem(dp, NC)
    yh = lax.rem(dp // NC, NYH)
    z = dp // (NC * NYH)
    x, yl = ctx // NYL, lax.rem(ctx, NYL)
    here = yh * NYL + yl
    gw = q_ref.shape[1] // GROUPS
    dout = cot_ref.shape[1]
    dx = dout // NX
    zg = NZ // GROUPS
    rows = gw // (zg * NYH * NC)
    yw = dx // NYL
    yc = max(yw, 128)

    right = (dp, lax.rem(ctx + 1, n_ctx))
    left = (dp, lax.rem(ctx + n_ctx - 1, n_ctx))
    sibling = (dp - core + (NC - 1 - core), ctx)

    def at_x(d):
        return (dp, lax.rem(x + d, NX) * NYL + yl)

    def at_z(zz):
        return ((zz * NYH + yh) * NC + core, ctx)

    def at_y(k):
        return ((z * NYH + k // NYL) * NC + core, x * NYL + lax.rem(k, NYL))

    barrier = pltpu.get_barrier_semaphore()

    def hello(device):
        pl.semaphore_signal(barrier, inc=1, device_id=device, device_id_type=MESH)

    hello(right)
    hello(left)
    hello(sibling)
    for d in range(1, NX):
        hello(at_x(d))
    if NZ > 1:
        @pl.loop(1, NZ)
        def _(d):
            hello(at_z(lax.rem(z + d, NZ)))
    if NYH * NYL > 1:
        @pl.loop(1, NYH * NYL)
        def _(d):
            hello(at_y(lax.rem(here + d, NYH * NYL)))

    clips[2] = jnp.full((8, 128), clip_ref[0, 0], jnp.int32)
    for g in range(GROUPS):
        kcat[g, 2 * BLOCK :, :] = k_ref[:, g * gw : (g + 1) * gw]
        vcat[g, 2 * BLOCK :, :] = v_ref[:, g * gw : (g + 1) * gw]
    pl.semaphore_wait(barrier, 3 + (NX - 1) + (NZ - 1) + (NYH * NYL - 1))

    sends = []

    def remote(src, dst, send_sem, recv_sem, device):
        return pltpu.make_async_remote_copy(
            src_ref=src, dst_ref=dst, send_sem=send_sem, recv_sem=recv_sem,
            device_id=device, device_id_type=MESH,
        )

    def start(copy):
        copy.start()
        sends.append(copy)
        return copy

    def halo(g, hop):
        low = (1 - hop) * BLOCK
        part = []
        for number, cat in enumerate((kcat, vcat)):
            part.append(
                remote(
                    cat.at[g, pl.ds(low + BLOCK, BLOCK), :],
                    cat.at[g, pl.ds(low, BLOCK), :],
                    halo_sem.at[0, hop, g, number],
                    halo_sem.at[1, hop, g, number],
                    right,
                )
            )
        return part

    def clip_hop(hop):
        return remote(
            clips.at[2 - hop], clips.at[1 - hop], clip_sem.at[0, hop], clip_sem.at[1, hop], right
        )

    first = [clip_hop(0)]
    hops = [[halo(g, 0) for g in range(GROUPS)], [halo(g, 1) for g in range(GROUPS)]]
    start(first[0])
    for g in range(GROUPS):
        for copy in hops[0][g]:
            start(copy)

    def d_attended(g):
        cols = slice(g * gw, (g + 1) * gw)
        da_buf[:, cols] = dot_nn(cot_ref[...], w_ref[:, cols]).astype(BF16)

    first[0].wait_recv()
    second = start(clip_hop(1))
    for g in range(GROUPS):
        d_attended(g)
        for number in range(2):
            hops[0][g][number].wait_recv()
            start(hops[1][g][number])
    second.wait_recv()

    row = lax.broadcasted_iota(jnp.int32, (BLOCK, BLOCK), 0)
    col = lax.broadcasted_iota(jnp.int32, (BLOCK, BLOCK), 1)
    own_clip = clips[2, 0:1, :]
    for part in range(3):
        shown = clips[part, 0:1, :] == own_clip
        shown = jnp.broadcast_to(shown, (BLOCK, BLOCK))
        if part == 0:
            shown = shown & (col > row)
        if part == 2:
            shown = shown & (col <= row)
        shown = shown & (col + (ctx + part - 2) * BLOCK >= 0)
        term = jnp.where(shown, 0.0, -1e30).astype(F32)
        cols = slice(part * BLOCK, (part + 1) * BLOCK)
        bias[0:BLOCK, cols] = term
        bias[BLOCK:, cols] = term

    scaling = 1.0 / math.sqrt(HDIM)
    lane = lax.broadcasted_iota(jnp.int32, (BLOCK, PAIR), 1)
    low_head = lane < HDIM

    def stacked(value):
        return jnp.concatenate(
            [jnp.where(low_head, value, 0.0), jnp.where(low_head, 0.0, value)], axis=0
        )

    def picked(value):
        return jnp.where(low_head, value[:BLOCK], value[BLOCK:])

    def attention(g):
        @pl.loop(0, gw // PAIR)
        def _(p):
            lanes = pl.ds(pl.multiple_of(p * PAIR, PAIR), PAIR)
            whole = pl.ds(pl.multiple_of(g * gw + p * PAIR, PAIR), PAIR)
            q2 = stacked(q_ref[:, whole].astype(F32) * scaling).astype(BF16)
            da_f32 = stacked(da_buf[:, whole].astype(F32))
            da2 = da_f32.astype(BF16)
            keys = kcat[g, :, lanes]
            values = vcat[g, :, lanes]
            scores = dot_nt(q2, keys) + bias[...]
            top = jnp.max(scores, axis=1, keepdims=True)
            powers = jnp.exp(scores - top)
            probs = powers * (1.0 / jnp.sum(powers, axis=1, keepdims=True))
            weights = probs.astype(BF16)
            attended = picked(dot_nn(weights, values)).astype(BF16)
            att_buf[:, whole] = attended
            att_f32 = attended.astype(F32)
            delta = jnp.sum(da_f32 * jnp.concatenate([att_f32, att_f32], axis=0), axis=1, keepdims=True)
            d_weights = dot_nt(da2, values)
            d_scores = (probs * (d_weights - delta)).astype(BF16)
            dq_ref[:, whole] = (picked(dot_nn(d_scores, keys)) * scaling).astype(BF16)
            key_part = dot_tn(d_scores, q2)
            value_part = dot_tn(weights, da2)
            for part, far, near, own in (
                (key_part, far_k, near_k, own_k),
                (value_part, far_v, near_v, own_v),
            ):
                far[g, :, lanes] = part[0:BLOCK].astype(BF16)
                near[g, :, lanes] = part[BLOCK : 2 * BLOCK]
                own[g, :, lanes] = part[2 * BLOCK :]

    def far_back(g):
        return [
            remote(far.at[g], into.at[g], back_sem.at[0, 0, g, n], back_sem.at[1, 0, g, n], left)
            for n, (far, into) in enumerate(((far_k, in_far_k), (far_v, in_far_v)))
        ]

    def near_back(g):
        return [
            remote(mid.at[g], into.at[g], back_sem.at[0, 1, g, n], back_sem.at[1, 1, g, n], left)
            for n, (mid, into) in enumerate(((sum_k, in_near_k), (sum_v, in_near_v)))
        ]

    far_copies = [far_back(g) for g in range(GROUPS)]
    near_copies = [near_back(g) for g in range(GROUPS)]

    def relay_back(g):
        for n, (near, into, mid) in enumerate(((near_k, in_far_k, sum_k), (near_v, in_far_v, sum_v))):
            far_copies[g][n].wait_recv()
            mid[g] = (near[g] + into[g].astype(F32)).astype(BF16)
            start(near_copies[g][n])

    def finish_back(g):
        cols = slice(g * gw, (g + 1) * gw)
        for n, (own, into, result) in enumerate(((own_k, in_near_k, dk_ref), (own_v, in_near_v, dv_ref))):
            near_copies[g][n].wait_recv()
            result[:, cols] = (own[g] + into[g].astype(F32)).astype(BF16)

    half = gw // NC

    def a_copy(g):
        return remote(
            g_buf.at[NC - 1 - core, g], a_in.at[g], a_sem.at[0, g], a_sem.at[1, g], sibling
        )

    a_copies = [a_copy(g) for g in range(GROUPS)]

    def weight_terms(g):
        for part in range(NX):
            terms = dot_tn(
                att_buf[:, g * gw : (g + 1) * gw], cot_ref[:, part * dx : (part + 1) * dx]
            ).reshape(zg * NYH, NC, rows, dx)
            for number in range(NC):
                g_buf[number, g, part] = terms[:, number].reshape(half, dx).astype(BF16)
        start(a_copies[g])

    def b_copy(g, d):
        return remote(
            b_buf.at[g, lax.rem(x + d, NX)], b_in.at[g, d - 1],
            b_sem.at[0, g, d - 1], b_sem.at[1, g, d - 1], at_x(d),
        )

    b_copies = [[b_copy(g, d) for d in range(1, NX)] for g in range(GROUPS)]

    def after_core(g):
        a_copies[g].wait_recv()
        for part in range(NX):
            b_buf[g, part] = (g_buf[core, g, part].astype(F32) + a_in[g, part].astype(F32)).astype(BF16)
        for copy in b_copies[g]:
            start(copy)

    def z_copy(g, j):
        return remote(
            z_buf.at[g, j], z_in.at[z], z_send.at[g * zg + j], z_recv.at[z], at_z(g * zg + j)
        )

    def after_x(g):
        total = b_buf[g, x].astype(F32)
        for d in range(1, NX):
            b_copies[g][d - 1].wait_recv()
            total = total + b_in[g, d - 1].astype(F32)
        z_buf[g] = total.reshape(zg, half // zg, dx).astype(BF16)
        for j in range(zg):
            @pl.when(z != g * zg + j)
            def _():
                z_copy(g, j).start()

            @pl.when(z == g * zg + j)
            def _():
                z_in[z] = z_buf[g, j]

    def y_copy(k):
        return remote(
            y_buf.at[pl.ds((k // NYL) * rows, rows), pl.ds(((k % NYL) * yw) // yc * yc, yc)],
            y_in.at[here], y_send.at[k], y_recv.at[here], at_y(k),
        )

    def after_z():
        @pl.loop(0, NZ)
        def _(s):
            @pl.when(s != z)
            def _():
                remote(z_buf.at[0, 0], z_in.at[s], z_send.at[s], z_recv.at[s], at_z(s)).wait_recv()
        total = z_in[0].astype(F32)
        for s in range(1, NZ):
            total = total + z_in[s].astype(F32)
        y_buf[...] = total
        for k in range(NYH * NYL):
            @pl.when(k != here)
            def _():
                y_copy(k).start()

            @pl.when(k == here)
            def _():
                low = ((k % NYL) * yw) // yc * yc
                y_in[here] = y_buf[(k // NYL) * rows : (k // NYL + 1) * rows, low : low + yc]

    def after_y():
        @pl.loop(0, NYH * NYL)
        def _(s):
            @pl.when(s != here)
            def _():
                remote(
                    y_buf.at[pl.ds(0, rows), pl.ds(0, yc)], y_in.at[s], y_send.at[s], y_recv.at[s], at_y(s)
                ).wait_recv()
        total = y_in[0]
        for s in range(1, NYH * NYL):
            total = total + y_in[s]
        t_buf[...] = total.T
        offset = lax.rem(yl * yw, yc)
        wg_ref[...] = t_buf[pl.ds(pl.multiple_of(offset, 8), yw), :]

    def project(part):
        piece = slice(part * dx, (part + 1) * dx)
        out_ref[:, piece] = dot_nt(att_buf[...], w_ref[piece, :]).astype(BF16)

    for g in range(GROUPS):
        for copy in hops[1][g]:
            copy.wait_recv()
        attention(g)
        for copy in far_copies[g]:
            start(copy)
        weight_terms(g)
        if g >= 1:
            relay_back(g - 1)
            after_core(g - 1)
        if g >= 2:
            after_x(g - 2)
    after_core(GROUPS - 1)
    relay_back(GROUPS - 1)
    after_x(GROUPS - 2)
    for part in range(NX):
        project(part)
    after_x(GROUPS - 1)
    for g in range(GROUPS - 1):
        finish_back(g)
    after_z()
    finish_back(GROUPS - 1)
    after_y()

    for copy in sends:
        copy.wait_send()

    @pl.loop(0, NZ)
    def _(s):
        @pl.when(s != z)
        def _():
            remote(z_buf.at[0, 0], z_in.at[s], z_send.at[s], z_recv.at[s], at_z(s)).wait_send()

    @pl.loop(0, NYH * NYL)
    def _(s):
        @pl.when(s != here)
        def _():
            remote(
                y_buf.at[pl.ds(0, rows), pl.ds(0, yc)], y_in.at[s], y_send.at[s], y_recv.at[s], at_y(s)
            ).wait_send()


def per_device(queries, key_states, value_states, out_cotangent, out_weight, block_clip):
    steps, width = queries.shape[1:]
    dout = out_cotangent.shape[2]
    gw = width // GROUPS
    dx = dout // NX
    zg = NZ // GROUPS
    rows = gw // (zg * NYH * NC)
    half = gw // NC
    yw = dx // NYL
    yc = max(yw, 128)
    ny = NYH * NYL
    shape = jax.ShapeDtypeStruct
    vmem = pltpu.VMEM
    dma = pltpu.SemaphoreType.DMA
    group_bf16 = vmem((GROUPS, BLOCK, gw), BF16)
    group_f32 = vmem((GROUPS, BLOCK, gw), F32)
    out, dq, dk, dv, wg = pl.pallas_call(
        kernel,
        out_shape=(
            shape((steps, dout), BF16),
            shape((steps, width), BF16),
            shape((steps, width), BF16),
            shape((steps, width), BF16),
            shape((yw, rows), F32),
        ),
        in_specs=[pl.BlockSpec(memory_space=pltpu.SMEM)] + [pl.BlockSpec(memory_space=vmem)] * 5,
        out_specs=tuple([pl.BlockSpec(memory_space=vmem)] * 5),
        scratch_shapes=[
            vmem((GROUPS, WIN + BLOCK, gw), BF16),
            vmem((GROUPS, WIN + BLOCK, gw), BF16),
            vmem((3, 8, 128), jnp.int32),
            vmem((2 * BLOCK, WIN + BLOCK), F32),
            vmem((steps, width), BF16),
            vmem((steps, width), BF16),
            group_f32, group_f32, group_f32, group_f32,
            group_bf16, group_bf16, group_bf16, group_bf16,
            group_bf16, group_bf16, group_bf16, group_bf16,
            vmem((NC, GROUPS, NX, half, dx), BF16),
            vmem((GROUPS, NX, half, dx), BF16),
            vmem((GROUPS, NX, half, dx), BF16),
            vmem((GROUPS, max(NX - 1, 1), half, dx), BF16),
            vmem((GROUPS, zg, half // zg, dx), BF16),
            vmem((NZ, half // zg, dx), BF16),
            vmem((half // zg, dx), F32),
            vmem((ny, rows, yc), F32),
            vmem((yc, rows), F32),
            dma((2, 2)),
            dma((2, 2, GROUPS, 2)),
            dma((2, 2, GROUPS, 2)),
            dma((2, GROUPS)),
            dma((2, GROUPS, max(NX - 1, 1))),
            dma((NZ,)),
            dma((NZ,)),
            dma((ny,)),
            dma((ny,)),
        ],
        compiler_params=pltpu.CompilerParams(
            collective_id=0, has_side_effects=True, vmem_limit_bytes=48 * 1024 * 1024
        ),
    )(block_clip, queries[0], key_states[0], value_states[0], out_cotangent[0], out_weight)
    return out[None], dq[None], dk[None], dv[None], wg


def solution(mesh):
    tokens = P("dp", "ctx", None)
    return jax.shard_map(
        per_device,
        mesh=mesh,
        in_specs=(tokens, tokens, tokens, tokens, P(), P("dp", "ctx")),
        out_specs=(tokens, tokens, tokens, tokens, P("ctx", "dp")),
        check_vma=False,
    )
```

```python
import math

import jax
import jax.numpy as jnp
from jax import lax
from jax.experimental import pallas as pl
from jax.experimental.pallas import tpu as pltpu
from jax.sharding import PartitionSpec as P

HDIM = 64
BLOCK = 128
WIN = 256
GROUPS = 3
PAIR = 2 * HDIM
STAT = 32

NZ, NYH, NC = 12, 2, 2
NX, NYL = 4, 4

BF16 = jnp.bfloat16
F32 = jnp.float32
MESH = pl.DeviceIdType.MESH


def dot_nn(a, b):
    return lax.dot_general(a, b, (((1,), (0,)), ((), ())), preferred_element_type=F32)


def dot_nt(a, b):
    return lax.dot_general(a, b, (((1,), (1,)), ((), ())), preferred_element_type=F32)


def dot_tn(a, b):
    return lax.dot_general(a, b, (((0,), (0,)), ((), ())), preferred_element_type=F32)


def kernel(
    clip_ref, q_ref, k_ref, v_ref, cot_ref, w_ref,
    out_hbm, dq_hbm, dk_hbm, dv_hbm, wg_hbm,
    out_ref, dq_ref, dk_ref, dv_ref, wg_ref,
    q_buf, cot_buf, w_buf, kcat, vcat, clips, bias, da_buf, att_buf,
    own_k, own_v, qcat, dcat, next_clips, next_bias, stat_cols, stat_own, stat_in,
    g_buf, a_in, b_buf, b_in, y_out, y_in, z_src, z_in,
    in_sem, own_sem, res_sem, clip_sem, halo_sem, next_sem, stat_sem, a_sem, b_sem, z_send, z_recv, y_send, y_recv,
):
    dp, ctx = lax.axis_index("dp"), lax.axis_index("ctx")
    n_ctx = NX * NYL
    core = lax.rem(dp, NC)
    yh = lax.rem(dp // NC, NYH)
    z = dp // (NC * NYH)
    x, yl = ctx // NYL, lax.rem(ctx, NYL)
    here = yh * NYL + yl
    gw = q_ref.shape[1] // GROUPS
    dout = cot_ref.shape[1]
    dx = dout // NX
    zg = NZ // GROUPS
    rows = gw // (zg * NYH * NC)
    yw = dx // NYL
    yc = max(yw, 128)
    sharers = yc // yw
    zh = zg // sharers
    side = lax.rem(yl, sharers)

    right = (dp, lax.rem(ctx + 1, n_ctx))
    left = (dp, lax.rem(ctx + n_ctx - 1, n_ctx))
    sibling = (dp - core + (NC - 1 - core), ctx)

    def at_x(d):
        return (dp, lax.rem(x + d, NX) * NYL + yl)

    def at_z(zz, n):
        return ((zz * NYH + yh) * NC + core, ctx - side + n)

    def at_y(k):
        return ((z * NYH + k // NYL) * NC + core, x * NYL + lax.rem(k, NYL))

    stores = []

    def write(src, dst):
        copy = pltpu.make_async_copy(src, dst, res_sem.at[len(stores)])
        copy.start()
        stores.append(copy)

    loads = [
        pltpu.make_async_copy(src, dst, in_sem.at[n])
        for n, (src, dst) in enumerate(((cot_ref, cot_buf), (w_ref, w_buf), (q_ref, q_buf)))
    ]
    own_loads = [
        [
            pltpu.make_async_copy(
                src.at[:, pl.ds(g * gw, gw)], cat.at[g, pl.ds(2 * BLOCK, BLOCK), :], own_sem.at[g, n]
            )
            for n, (src, cat) in enumerate(((k_ref, kcat), (v_ref, vcat)))
        ]
        for g in range(GROUPS)
    ]
    for copy in loads:
        copy.start()
    for pair in own_loads:
        for copy in pair:
            copy.start()
    clips[2] = jnp.full((8, 128), clip_ref[0, 0], jnp.int32)
    next_clips[0] = jnp.full((8, 128), clip_ref[0, 0], jnp.int32)

    barrier = pltpu.get_barrier_semaphore()

    def hello(device):
        pl.semaphore_signal(barrier, inc=1, device_id=device, device_id_type=MESH)

    hello(right)
    hello(left)
    hello(sibling)
    for d in range(1, NX):
        hello(at_x(d))
    @pl.loop(0, NZ)
    def _(d):
        zz = lax.rem(z + d, NZ)
        for n in range(sharers):
            @pl.when((zz != z) | (side != n))
            def _():
                hello(at_z(zz, n))
    if NYH * NYL > 1:
        @pl.loop(1, NYH * NYL)
        def _(d):
            hello(at_y(lax.rem(here + d, NYH * NYL)))

    pl.semaphore_wait(barrier, 3 + (NX - 1) + (sharers * NZ - 1) + (NYH * NYL - 1))

    sends = []

    def remote(src, dst, send_sem, recv_sem, device):
        return pltpu.make_async_remote_copy(
            src_ref=src, dst_ref=dst, send_sem=send_sem, recv_sem=recv_sem,
            device_id=device, device_id_type=MESH,
        )

    def start(copy):
        copy.start()
        sends.append(copy)
        return copy

    def halo(g, hop):
        low = (1 - hop) * BLOCK
        part = []
        for number, (src, cat) in enumerate(((k_ref, kcat), (v_ref, vcat))):
            part.append(
                remote(
                    src.at[:, pl.ds(g * gw, gw)] if hop == 0 else cat.at[g, pl.ds(low + BLOCK, BLOCK), :],
                    cat.at[g, pl.ds(low, BLOCK), :],
                    halo_sem.at[0, hop, g, number],
                    halo_sem.at[1, hop, g, number],
                    right,
                )
            )
        return part

    def next_halo(g, hop):
        cols = pl.ds(g * gw, gw)
        return [
            remote(
                own.at[:, cols] if hop == 0 else cat.at[g, pl.ds(0, BLOCK), :],
                cat.at[g, pl.ds(hop * BLOCK, BLOCK), :],
                next_sem.at[0, hop, g, number],
                next_sem.at[1, hop, g, number],
                left,
            )
            for number, (own, cat) in enumerate(((q_ref, qcat), (da_buf, dcat)))
        ]

    def clip_hop(hop):
        return [
            remote(
                clips.at[2 - hop], clips.at[1 - hop],
                clip_sem.at[0, hop, 0], clip_sem.at[1, hop, 0], right,
            ),
            remote(
                next_clips.at[hop], next_clips.at[hop + 1],
                clip_sem.at[0, hop, 1], clip_sem.at[1, hop, 1], left,
            ),
        ]

    clip_hops = [clip_hop(0), clip_hop(1)]
    hops = [[halo(g, hop) for g in range(GROUPS)] for hop in range(2)]
    next_hops = [[next_halo(g, hop) for g in range(GROUPS)] for hop in range(2)]
    for copy in clip_hops[0]:
        start(copy)
    for g in range(GROUPS):
        for copy in hops[0][g]:
            start(copy)

    def d_attended(g):
        cols = slice(g * gw, (g + 1) * gw)
        da_buf[:, cols] = dot_nn(cot_buf[...], w_buf[:, cols]).astype(BF16)

    loads[0].wait()
    loads[1].wait()
    for n in range(2):
        clip_hops[0][n].wait_recv()
        start(clip_hops[1][n])
    for g in range(GROUPS):
        d_attended(g)
        for number in range(2):
            hops[0][g][number].wait_recv()
            start(hops[1][g][number])
        for copy in next_hops[0][g]:
            start(copy)
    for n in range(2):
        clip_hops[1][n].wait_recv()
    loads[2].wait()
    for pair in own_loads:
        for copy in pair:
            copy.wait()

    row = lax.broadcasted_iota(jnp.int32, (BLOCK, BLOCK), 0)
    col = lax.broadcasted_iota(jnp.int32, (BLOCK, BLOCK), 1)
    own_clip = clips[2, 0:1, :]
    for part in range(3):
        shown = clips[part, 0:1, :] == own_clip
        shown = jnp.broadcast_to(shown, (BLOCK, BLOCK))
        if part == 0:
            shown = shown & (col > row)
        if part == 2:
            shown = shown & (col <= row)
        shown = shown & (col + (ctx + part - 2) * BLOCK >= 0)
        term = jnp.where(shown, 0.0, -1e30).astype(F32)
        cols = slice(part * BLOCK, (part + 1) * BLOCK)
        bias[0:BLOCK, cols] = term
        bias[BLOCK:, cols] = term

    for part in range(2):
        shown = next_clips[part + 1, 0:1, :] == next_clips[0, 0:1, :]
        shown = jnp.broadcast_to(shown, (BLOCK, BLOCK))
        if part == 1:
            shown = shown & (row > col)
        shown = shown & (col * 0 + ctx + part + 1 < n_ctx)
        term = jnp.where(shown, 0.0, -1e30).astype(F32)
        cols = slice(part * BLOCK, (part + 1) * BLOCK)
        next_bias[0:BLOCK, cols] = term
        next_bias[BLOCK:, cols] = term

    stat_cols[...] = jnp.zeros_like(stat_cols)
    scaling = 1.0 / math.sqrt(HDIM)
    lane = lax.broadcasted_iota(jnp.int32, (BLOCK, PAIR), 1)
    low_head = lane < HDIM

    def stacked(value):
        return jnp.concatenate(
            [jnp.where(low_head, value, 0.0), jnp.where(low_head, 0.0, value)], axis=0
        )

    def picked(value):
        return jnp.where(low_head, value[:BLOCK], value[BLOCK:])

    def attention(g):
        @pl.loop(0, gw // PAIR)
        def _(p):
            lanes = pl.ds(pl.multiple_of(p * PAIR, PAIR), PAIR)
            whole = pl.ds(pl.multiple_of(g * gw + p * PAIR, PAIR), PAIR)
            q2 = stacked(q_buf[:, whole].astype(F32) * scaling).astype(BF16)
            da_f32 = stacked(da_buf[:, whole].astype(F32))
            da2 = da_f32.astype(BF16)
            keys = kcat[g, :, lanes]
            values = vcat[g, :, lanes]
            scores = dot_nt(q2, keys) + bias[...]
            top = jnp.max(scores, axis=1, keepdims=True)
            powers = jnp.exp(scores - top)
            total = jnp.sum(powers, axis=1, keepdims=True)
            probs = powers * (1.0 / total)
            weights = probs.astype(BF16)
            attended = picked(dot_nn(weights, values)).astype(BF16)
            att_buf[:, whole] = attended
            att_f32 = attended.astype(F32)
            delta = jnp.sum(da_f32 * jnp.concatenate([att_f32, att_f32], axis=0), axis=1, keepdims=True)
            log_total = top + jnp.log(total)
            d_weights = dot_nt(da2, values)
            d_scores = (probs * (d_weights - delta)).astype(BF16)
            dq_ref[:, whole] = (picked(dot_nn(d_scores, keys)) * scaling).astype(BF16)
            own_k[g, :, lanes] = dot_tn(d_scores[:, 2 * BLOCK :], q2)
            own_v[g, :, lanes] = dot_tn(weights[:, 2 * BLOCK :], da2)
            head = 2 * (g * (gw // PAIR) + p)
            stats = stat_cols[...]
            for n in range(2):
                part = slice(n * BLOCK, (n + 1) * BLOCK)
                stats = jnp.where(lane == head + n, log_total[part], stats)
                stats = jnp.where(lane == head + n + STAT, delta[part], stats)
            stat_cols[...] = stats

    def stat_copy(hop):
        return remote(
            stat_own if hop == 0 else stat_in.at[0], stat_in.at[hop],
            stat_sem.at[0, hop], stat_sem.at[1, hop], left,
        )

    stat_hops = [stat_copy(0), stat_copy(1)]

    def send_stats():
        stat_own[...] = stat_cols[...].T[: 2 * STAT]
        start(stat_hops[0])

    def relay(copies, later):
        for copy, after in zip(copies, later):
            copy.wait_recv()
            start(after)

    def key_side(g):
        for copy in next_hops[1][g]:
            copy.wait_recv()

        @pl.loop(0, gw // PAIR)
        def _(p):
            lanes = pl.ds(pl.multiple_of(p * PAIR, PAIR), PAIR)
            whole = pl.ds(pl.multiple_of(g * gw + p * PAIR, PAIR), PAIR)
            head = 2 * (g * (gw // PAIR) + p)

            def spread(offset):
                parts = []
                for n in range(2):
                    line = jnp.concatenate(
                        [stat_in[hop, pl.ds(head + n + offset, 1), :] for hop in range(2)], axis=1
                    )
                    parts.append(jnp.broadcast_to(line, (BLOCK, 2 * BLOCK)))
                return jnp.concatenate(parts, axis=0)

            k2 = stacked(kcat[g, 2 * BLOCK :, lanes].astype(F32) * scaling).astype(BF16)
            v2 = stacked(vcat[g, 2 * BLOCK :, lanes].astype(F32)).astype(BF16)
            next_q = qcat[g, :, lanes]
            next_d = dcat[g, :, lanes]
            probs = jnp.exp(dot_nt(k2, next_q) + next_bias[...] - spread(0))
            weights = probs.astype(BF16)
            d_scores = (probs * (dot_nt(v2, next_d) - spread(STAT))).astype(BF16)
            key_part = picked(dot_nn(d_scores, next_q)) * scaling
            value_part = picked(dot_nn(weights, next_d))
            dk_ref[:, whole] = (own_k[g, :, lanes] + key_part).astype(BF16)
            dv_ref[:, whole] = (own_v[g, :, lanes] + value_part).astype(BF16)

        cols = pl.ds(g * gw, gw)
        write(dk_ref.at[:, cols], dk_hbm.at[:, cols])
        write(dv_ref.at[:, cols], dv_hbm.at[:, cols])

    half = gw // NC

    def a_copy(g):
        return remote(
            g_buf.at[NC - 1 - core, g], a_in.at[g], a_sem.at[0, g], a_sem.at[1, g], sibling
        )

    a_copies = [a_copy(g) for g in range(GROUPS)]

    def weight_terms(g):
        for part in range(NX):
            terms = dot_tn(
                att_buf[:, g * gw : (g + 1) * gw], cot_buf[:, part * dx : (part + 1) * dx]
            ).reshape(zg * NYH, NC, rows, dx)
            for number in range(NC):
                g_buf[number, g, part] = terms[:, number].reshape(half, dx).astype(BF16)
        start(a_copies[g])

    def b_copy(g, d):
        return remote(
            b_buf.at[g, lax.rem(x + d, NX)], b_in.at[g, d - 1],
            b_sem.at[0, g, d - 1], b_sem.at[1, g, d - 1], at_x(d),
        )

    b_copies = [[b_copy(g, d) for d in range(1, NX)] for g in range(GROUPS)]

    def after_core(g):
        a_copies[g].wait_recv()
        for part in range(NX):
            b_buf[g, part] = (g_buf[core, g, part].astype(F32) + a_in[g, part].astype(F32)).astype(BF16)
        for copy in b_copies[g]:
            start(copy)

    def y_copy(g, k):
        return remote(y_out.at[g, k], y_in.at[g, here], y_send.at[g, k], y_recv.at[g, here], at_y(k))

    def y_arrival(g, s):
        return remote(y_out.at[g, s], y_in.at[g, s], y_send.at[g, s], y_recv.at[g, s], at_y(s))

    def after_x(g):
        total = b_buf[g, x].astype(F32)
        for d in range(1, NX):
            b_copies[g][d - 1].wait_recv()
            total = total + b_in[g, d - 1].astype(F32)
        total = total.reshape(zg, NYH, rows, dx)
        for k in range(NYH * NYL):
            high, low = (k % NYL) // sharers, k % sharers
            piece = total[low * zh : (low + 1) * zh, k // NYL, :, high * yc : (high + 1) * yc]
            y_out[g, k] = piece.reshape(zh * rows, yc).astype(BF16)

            @pl.when(k != here)
            def _():
                y_copy(g, k).start()

            @pl.when(k == here)
            def _():
                y_in[g, here] = y_out[g, k]

    def z_copy(g, j, n):
        zz = g * zg + side * zh + j
        return remote(z_src.at[g, j], z_in.at[z], z_send.at[g, j, n], z_recv.at[z], at_z(zz, n))

    def after_y(g):
        @pl.loop(0, NYH * NYL)
        def _(s):
            @pl.when(s != here)
            def _():
                y_arrival(g, s).wait_recv()

        total = y_in[g, 0].astype(F32)
        for s in range(1, NYH * NYL):
            total = total + y_in[g, s].astype(F32)
        for j in range(zh):
            z_src[g, j] = total[j * rows : (j + 1) * rows]
            for n in range(sharers):
                mine = (g * zg + side * zh + j == z) & (side == n)

                @pl.when(jnp.logical_not(mine))
                def _():
                    z_copy(g, j, n).start()

                @pl.when(mine)
                def _():
                    z_in[z] = z_src[g, j]

    def after_z():
        source_side = lax.rem(z, zg) // zh

        @pl.loop(0, NZ)
        def _(s):
            @pl.when((s != z) | (source_side != side))
            def _():
                remote(
                    z_src.at[0, 0], z_in.at[s], z_send.at[0, 0, 0], z_recv.at[s], at_z(s, source_side)
                ).wait_recv()
        total = z_in[0]
        for s in range(1, NZ):
            total = total + z_in[s]
        mine = total[:, 0:yw]
        for n in range(1, sharers):
            mine = jnp.where(side == n, total[:, n * yw : (n + 1) * yw], mine)
        wg_ref[...] = mine
        write(wg_ref, wg_hbm)

    def project(part):
        piece = slice(part * dx, (part + 1) * dx)
        out_ref[:, piece] = dot_nt(att_buf[...], w_buf[piece, :]).astype(BF16)

    for g in range(GROUPS):
        for copy in hops[1][g]:
            copy.wait_recv()
        attention(g)
        cols = pl.ds(g * gw, gw)
        write(dq_ref.at[:, cols], dq_hbm.at[:, cols])
        if g >= 1:
            relay(next_hops[0][g - 1], next_hops[1][g - 1])
        weight_terms(g)
        if g >= 1:
            after_core(g - 1)
        if g >= 2:
            after_x(g - 2)
    send_stats()
    after_core(GROUPS - 1)
    relay(next_hops[0][GROUPS - 1], next_hops[1][GROUPS - 1])
    after_x(1)
    after_y(0)
    relay(stat_hops[:1], stat_hops[1:])
    after_x(2)
    for part in range(NX):
        project(part)
    write(out_ref, out_hbm)
    after_y(1)
    after_y(2)
    stat_hops[1].wait_recv()
    key_side(0)
    after_z()
    key_side(1)
    key_side(2)

    for copy in stores:
        copy.wait()
    for copy in sends:
        copy.wait_send()

    for g in range(GROUPS):
        @pl.loop(0, NYH * NYL)
        def _(s):
            @pl.when(s != here)
            def _():
                y_arrival(g, s).wait_send()

        for j in range(zh):
            for n in range(sharers):
                @pl.when((g * zg + side * zh + j != z) | (side != n))
                def _():
                    z_copy(g, j, n).wait_send()


def store(*refs):
    sources, results, held, sem = refs[:5], refs[5:10], refs[10:15], refs[15]
    loads = [pltpu.make_async_copy(sources[n], held[n], sem.at[0, n]) for n in range(5)]
    stores = [pltpu.make_async_copy(held[n], results[n], sem.at[1, n]) for n in range(5)]
    for copy in loads:
        copy.start()
    for load, copy in zip(loads, stores):
        load.wait()
        copy.start()
    for copy in stores:
        copy.wait()


def per_device(queries, key_states, value_states, out_cotangent, out_weight, block_clip):
    steps, width = queries.shape[1:]
    dout = out_cotangent.shape[2]
    gw = width // GROUPS
    dx = dout // NX
    zg = NZ // GROUPS
    rows = gw // (zg * NYH * NC)
    half = gw // NC
    yw = dx // NYL
    yc = max(yw, 128)
    ny = NYH * NYL
    zh = zg * yw // yc
    shape = jax.ShapeDtypeStruct
    vmem = pltpu.VMEM
    dma = pltpu.SemaphoreType.DMA
    group_f32 = vmem((GROUPS, BLOCK, gw), F32)
    out, dq, dk, dv, wg = pl.pallas_call(
        kernel,
        out_shape=(
            shape((steps, dout), BF16),
            shape((steps, width), BF16),
            shape((steps, width), BF16),
            shape((steps, width), BF16),
            shape((rows, yw), F32),
        ),
        in_specs=[pl.BlockSpec(memory_space=pltpu.SMEM)] + [pl.BlockSpec(memory_space=pltpu.HBM)] * 5,
        out_specs=tuple([pl.BlockSpec(memory_space=pltpu.HBM)] * 5),
        scratch_shapes=[
            vmem((steps, dout), BF16),
            vmem((steps, width), BF16),
            vmem((steps, width), BF16),
            vmem((steps, width), BF16),
            vmem((rows, yw), F32),
            vmem((steps, width), BF16),
            vmem((steps, dout), BF16),
            vmem((dout, width), BF16),
            vmem((GROUPS, WIN + BLOCK, gw), BF16),
            vmem((GROUPS, WIN + BLOCK, gw), BF16),
            vmem((3, 8, 128), jnp.int32),
            vmem((2 * BLOCK, WIN + BLOCK), F32),
            vmem((steps, width), BF16),
            vmem((steps, width), BF16),
            group_f32,
            group_f32,
            vmem((GROUPS, WIN, gw), BF16),
            vmem((GROUPS, WIN, gw), BF16),
            vmem((3, 8, 128), jnp.int32),
            vmem((2 * BLOCK, WIN), F32),
            vmem((BLOCK, BLOCK), F32),
            vmem((2 * STAT, BLOCK), F32),
            vmem((2, 2 * STAT, BLOCK), F32),
            vmem((NC, GROUPS, NX, half, dx), BF16),
            vmem((GROUPS, NX, half, dx), BF16),
            vmem((GROUPS, NX, half, dx), BF16),
            vmem((GROUPS, max(NX - 1, 1), half, dx), BF16),
            vmem((GROUPS, ny, zh * rows, yc), BF16),
            vmem((GROUPS, ny, zh * rows, yc), BF16),
            vmem((GROUPS, zh, rows, yc), F32),
            vmem((NZ, rows, yc), F32),
            dma((3,)),
            dma((GROUPS, 2)),
            dma((3 * GROUPS + 2,)),
            dma((2, 2, 2)),
            dma((2, 2, GROUPS, 2)),
            dma((2, 2, GROUPS, 2)),
            dma((2, 2)),
            dma((2, GROUPS)),
            dma((2, GROUPS, max(NX - 1, 1))),
            dma((GROUPS, zh, yc // yw)),
            dma((NZ,)),
            dma((GROUPS, ny)),
            dma((GROUPS, ny)),
        ],
        compiler_params=pltpu.CompilerParams(
            collective_id=0, has_side_effects=True, vmem_limit_bytes=60 * 1024 * 1024
        ),
    )(block_clip, queries[0], key_states[0], value_states[0], out_cotangent[0], out_weight)
    results = (out, dq, dk, dv, wg)
    out, dq, dk, dv, wg = pl.pallas_call(
        store,
        out_shape=tuple(shape(r.shape, r.dtype) for r in results),
        in_specs=[pl.BlockSpec(memory_space=pl.ANY)] * 5,
        out_specs=tuple([pl.BlockSpec(memory_space=pltpu.HBM)] * 5),
        scratch_shapes=[vmem(r.shape, r.dtype) for r in results] + [dma((2, 5))],
        compiler_params=pltpu.CompilerParams(vmem_limit_bytes=60 * 1024 * 1024),
    )(*results)
    return out[None], dq[None], dk[None], dv[None], wg.T


def solution(mesh):
    tokens = P("dp", "ctx", None)
    return jax.shard_map(
        per_device,
        mesh=mesh,
        in_specs=(tokens, tokens, tokens, tokens, P(), P("dp", "ctx")),
        out_specs=(tokens, tokens, tokens, tokens, P("ctx", "dp")),
        check_vma=False,
    )
```
